128 devices in a mesh: row: 8 (over y, z_hi), col: 16 (over z_lo, x, core).
Axes of the slice: x: 4, y: 4, z: 4 (z_hi: 2, z_lo: 2; z = z_hi * 2 + z_lo), core: 2. Of those that a mesh axis runs over, the one named last changes fastest.
Arguments:
- points: float32 [32, 49152], P(None, ('row', 'col')), may hold values from -6 to 6
- lengthscale: float32 [32], replicated, may hold values from 1.5 to 6
- outputscale: float32 [1], replicated, may hold values from 0.1 to 0.6
- noise: float32 [1], replicated, may hold values from 0.2 to 2
- rhs: float32 [17, 49152], P(None, ('row', 'col')), may hold values from -6 to 6
- iterate: float32 [17, 49152], P(None, ('row', 'col')), may hold values from -3 to 3
- residual: float32 [17, 49152], P(None, ('row', 'col')), may hold values from -27 to 27
- direction: float32 [17, 49152], P(None, ('row', 'col')), may hold values from -27 to 27
Outputs:
- iterate_next: float32 [17, 49152], P(None, ('row', 'col'))
- residual_next: float32 [17, 49152], P(None, ('row', 'col'))
- direction_next: float32 [17, 49152], P(None, ('row', 'col'))
- length_terms: float32 [32, 49152], P(None, ('row', 'col'))
The draws below stay inside these ranges and needn't reach their ends.
All inputs are finite; a program needn't handle non-finite values.
Results may differ from the reference program's by a relative error of at most 0.0003.
Values sent between devices are 32-bit elements; how exact they have to be, the bound alone decides.
A program may use at most 64 MiB of HBM per device.

```python
import math
import jax
import jax.numpy as jnp
from jax import lax

DIM = 32
PROBES = 16
SYSTEMS = 17
NPTS = 49152


def rising_rows(key, salt):
    key = jax.random.fold_in(key, salt)
    first_key, second_key = jax.random.split(key, 2)
    position = jnp.arange(NPTS, dtype=jnp.float32) / NPTS
    roughness = jnp.exp(0.5 * jax.random.uniform(second_key, (1, NPTS), jnp.float32, -1.0, 1.0))
    base_values = jax.random.truncated_normal(first_key, -5.0, 5.0, (SYSTEMS, NPTS), jnp.float32)
    row_scale = 10.0 ** (position - 0.5)
    return (base_values * row_scale[None, :] * roughness).astype(jnp.float32)


def draw_residual(key, part):
    return rising_rows(key, 11)


def draw_direction(key, part):
    return rising_rows(key, 23)


def block_scale(rng, dims, cuts, least, largest):
    def one(axis_at, shards_of):
        heights = jax.random.uniform(jax.random.fold_in(jax.random.fold_in(rng, 6), axis_at), (shards_of,), jnp.float32, least / len(cuts), largest / len(cuts))
        return jnp.repeat(jnp.exp(heights), dims[axis_at] // shards_of).reshape((-1,) + (1,) * (len(dims) - axis_at - 1))

    loudness = one(*cuts[0])
    for cut in cuts[1:]:
        loudness = loudness * one(*cut)
    return loudness


def bell_draw(own_key, dims, width, bound, cuts=(), held_as=jnp.bfloat16):
    drawn = width * jax.random.normal(own_key, dims, jnp.float32)
    if cuts:
        drawn = drawn * block_scale(own_key, dims, cuts, -0.22, 0.18)
    return jnp.clip(drawn, -bound, bound).astype(held_as)


def setup_inputs(seed: int = 0) -> dict:
    keys = jax.random.split(jax.random.key(seed), 9)
    points = bell_draw(keys[0], (DIM, NPTS), 1.0, 6.0, ((1, 128),), jnp.float32)
    lengthscale = jnp.clip(jnp.exp(jax.random.uniform(keys[1], (DIM,), jnp.float32, math.log(1.5), math.log(6.0))), 1.5, 6.0)
    outputscale = jnp.clip(jnp.exp(jax.random.uniform(keys[2], (1,), jnp.float32, math.log(0.1), math.log(0.6))), 0.1, 0.6)
    noise = jnp.clip(jnp.exp(jax.random.uniform(keys[3], (1,), jnp.float32, math.log(0.2), math.log(2.0))), 0.2, 2.0)
    rhs = bell_draw(keys[4], (SYSTEMS, NPTS), 1.0, 6.0, ((1, 128),), jnp.float32)
    iterate = bell_draw(keys[5], (SYSTEMS, NPTS), 0.5, 3.0, ((1, 128),), jnp.float32)
    residual = draw_residual(jax.random.fold_in(keys[8], 71), 0)
    direction = draw_direction(jax.random.fold_in(keys[8], 71), 0)
    return {"points": points, "lengthscale": lengthscale, "outputscale": outputscale, "noise": noise, "rhs": rhs, "iterate": iterate, "residual": residual, "direction": direction}


def tile_terms(row_scaled, row_iterate, col_scaled, col_direction, col_coeff, amplitude):
    row_sqnorm = jnp.sum(row_scaled * row_scaled, axis=0)
    col_sqnorm = jnp.sum(col_scaled * col_scaled, axis=0)
    inner_prod = jnp.einsum("dr,dc->rc", row_scaled, col_scaled, precision=lax.Precision.HIGHEST)
    kernel = amplitude * jnp.exp(-0.5 * (row_sqnorm[:, None] + col_sqnorm[None, :] - 2.0 * inner_prod))
    product = jnp.einsum("sc,rc->sr", col_direction, kernel, precision=lax.Precision.HIGHEST)
    weight = jnp.einsum("sr,sc->rc", row_iterate, col_coeff, precision=lax.Precision.HIGHEST)
    energy = kernel * weight
    stacked = jnp.concatenate([col_scaled, col_scaled * col_scaled], axis=0)
    moments = jnp.einsum("dc,rc->dr", stacked, energy, precision=lax.Precision.HIGHEST)
    dim_count = col_scaled.shape[0]
    row_total = jnp.sum(energy, axis=1)
    gradient = row_scaled * row_scaled * row_total[None, :] - 2.0 * row_scaled * moments[:dim_count] + moments[dim_count:]
    return product, gradient


def reference(points, lengthscale, outputscale, noise, rhs, iterate, residual, direction):
    scaled = points / lengthscale[:, None]
    coefficient = jnp.concatenate([iterate[:1], -rhs[1:] / PROBES], axis=0)
    amplitude = outputscale[0]
    row_width = math.gcd(NPTS, 512)
    starts = jnp.arange(NPTS // row_width, dtype=jnp.int32) * row_width

    def one_block(first_index):
        row_scaled = lax.dynamic_slice_in_dim(scaled, first_index, row_width, 1)
        row_iterate = lax.dynamic_slice_in_dim(iterate, first_index, row_width, 1)
        return tile_terms(row_scaled, row_iterate, scaled, direction, coefficient, amplitude)

    products, gradients = lax.map(one_block, starts)
    kernel_part = jnp.moveaxis(products, 0, 1).reshape(SYSTEMS, NPTS)
    grad_sum = jnp.moveaxis(gradients, 0, 1).reshape(DIM, NPTS)
    kernel_image = kernel_part + noise[0] * direction
    norm_now = jnp.sum(residual * residual, axis=1)
    curvature = jnp.sum(direction * kernel_image, axis=1)
    step_size = norm_now / curvature
    iterate_next = iterate + step_size[:, None] * direction
    residual_next = residual - step_size[:, None] * kernel_image
    norm_next = jnp.sum(residual_next * residual_next, axis=1)
    direction_next = residual_next + (norm_next / (norm_now + 1e-6))[:, None] * direction
    length_terms = 0.5 * grad_sum / lengthscale[:, None]
    return (iterate_next, residual_next, direction_next, length_terms)
```

```python
import functools
import math

import jax
import jax.numpy as jnp
from jax import lax
from jax.experimental import pallas as pl
from jax.experimental.pallas import tpu as pltpu
from jax.sharding import PartitionSpec as P

F32 = jnp.float32
BF16 = jnp.bfloat16
MESH = pl.DeviceIdType.MESH
LOG2E = math.log2(math.e)

ROWS = 8
CHIPS = 8
B = 384
UNIT_R = 2
CP = 72
RP = 56
DR = 24
MB = 48
MX = 176
MXL = 144
PART = 56


def dot(a, b):
    return lax.dot_general(a, b, (((1,), (0,)), ((), ())), preferred_element_type=F32)


def high(v):
    return v.astype(BF16).astype(F32)


def split(v):
    h = v.astype(BF16)
    return h, (v - h.astype(F32)).astype(BF16)


def norm_rows(first, second):
    lane = lax.broadcasted_iota(jnp.int32, (8, B), 0)
    s = -0.5 * jnp.sum(first * first + 2.0 * first * second, axis=0, keepdims=True)
    s0 = high(s)
    s1 = high(s - s0)
    s2 = s - s0 - s1
    parts = jnp.where(lane % 3 == 0, s0, jnp.where(lane % 3 == 1, s1, s2))
    return lane, parts


def prep_column(block, at, eye, fct, wct, dmat, xmat):
    y = block[0:32, :]
    yh = high(y)
    yl = high(y - yh)
    lane, parts = norm_rows(yh, yl)
    tail = jnp.where(lane < 3, parts, jnp.where(lane < 6, 1.0, 0.0))
    zeros = jnp.zeros((24, B), F32)
    c = block[32:56, :]
    ch = high(c)
    cl = c - ch
    feats = jnp.concatenate([yh, yl, yh, tail, zeros], axis=0).astype(BF16)
    wfeat = jnp.concatenate([ch, cl, ch, jnp.zeros((56, B), F32)], axis=0).astype(BF16)
    both = jnp.concatenate([feats, wfeat], axis=0)
    for j in range(B // 128):
        turned = lax.dot_general(
            eye, both[:, j * 128 : (j + 1) * 128], (((1,), (1,)), ((), ())), preferred_element_type=F32
        ).astype(BF16)
        rows = pl.ds(pl.multiple_of(at + j * 128, 128), 128)
        fct[rows, :] = turned[:, :128]
        wct[rows, :] = turned[:, 128:]
    cols = pl.ds(pl.multiple_of(at, 128), B)
    d = block[48:72, :]
    dh = high(d)
    dmat[:, cols] = jnp.concatenate([dh, d - dh], axis=0).astype(BF16)
    exact = yh + yl
    q = exact * exact
    q0 = high(q)
    q1 = high(q - q0)
    q2 = q - q0 - q1
    one = jnp.where(lax.broadcasted_iota(jnp.int32, (16, B), 0) == 0, 1.0, 0.0)
    xmat[:, cols] = jnp.concatenate([one, yh, yl, q0, q1, q2], axis=0).astype(BF16)


def prep_row(block, at, frm, wrm):
    y = block[0:32, :]
    yh = high(y)
    yl = high(y - yh)
    lane, parts = norm_rows(yh, yl)
    tail = jnp.where(lane < 3, 1.0, jnp.where(lane < 6, parts, 0.0))
    cols = pl.ds(pl.multiple_of(at, 128), B)
    frm[:, cols] = jnp.concatenate([yh, yh, yl, tail, jnp.zeros((24, B), F32)], axis=0).astype(BF16)
    c = block[32:56, :]
    ch = high(c)
    wrm[:, cols] = jnp.concatenate([ch, ch, c - ch, jnp.zeros((56, B), F32)], axis=0).astype(BF16)


ROW_STEPS = ((0, 0), (1, 0), (3, 0), (2, 0), (0, 1), (1, 1), (3, 1), (2, 1))
CHIP_STEPS = ((0, 0), (1, 0), (3, 0), (0, 1), (2, 0), (1, 1), (3, 1), (2, 1))


def kernel(
    points, lengths, amp, noise, rhs, iterate, residual, direction, ki_out, grad_out, stat_out,
    cpack, rpack, cbuf, rbuf, fct, wct, dmat, xmat, frm, wrm, accb, accx, part, red, statr, statc, tot,
    c_send, c_recv, f_send, f_recv, r_send, r_recv, p_send, p_recv, s_send, s_recv, t_send, t_recv,
):
    row = lax.axis_index("row")
    col = lax.axis_index("col")
    core = col % 2
    x = (col // 2) % 4
    z = col // 8
    mate = (row, z * 8 + x * 2 + (1 - core))

    def chip_to(k):
        dx, dz = CHIP_STEPS[k]
        return (row, ((z + dz) % 2) * 8 + ((x + dx) % 4) * 2 + core)

    def row_to(slot):
        dy, dz = ROW_STEPS[slot]
        return (((row // 2 + dy) % 4) * 2 + (row + dz) % 2, col)

    def row_from(slot):
        turn = slot % 4
        dy = turn + (turn // 2) * (1 - 2 * (turn % 2))
        return (((row // 2 + 4 - dy) % 4) * 2 + (row + slot // 4) % 2, col)

    barrier = pltpu.get_barrier_semaphore()
    for slot in range(1, ROWS):
        pl.semaphore_signal(barrier, inc=1, device_id=row_to(slot), device_id_type=MESH)
    for o in range(1, 2 * CHIPS):
        pl.semaphore_signal(barrier, inc=1, device_id=(row, (col + o) % 16), device_id_type=MESH)

    wide = jnp.broadcast_to(lengths[...], (32, 32))
    diagonal = lax.broadcasted_iota(jnp.int32, (32, 32), 0) == lax.broadcasted_iota(jnp.int32, (32, 32), 1)
    length = jnp.sum(jnp.where(diagonal, wide, 0.0), axis=1, keepdims=True)
    y = points[...] * (math.sqrt(LOG2E) / length)
    rpack[0:32, :] = y
    rpack[32:48, :] = iterate[1:17, :]
    rpack[48:49, :] = iterate[0:1, :]
    rpack[49:RP, :] = jnp.zeros((RP - 49, B), F32)
    cpack[0:32, :] = y
    cpack[32:48, :] = rhs[1:17, :] * (-1.0 / 16.0)
    cpack[48:49, :] = iterate[0:1, :]
    cpack[49:66, :] = direction[...]
    cpack[66:CP, :] = jnp.zeros((CP - 66, B), F32)
    pl.semaphore_wait(barrier, ROWS - 1 + 2 * CHIPS - 1)

    def send(src, dst, ssem, rsem, to):
        return pltpu.make_async_remote_copy(
            src_ref=src, dst_ref=dst, send_sem=ssem, recv_sem=rsem, device_id=to, device_id_type=MESH
        )

    def row_copy(slot, to):
        return send(rpack, rbuf.at[slot - 1], r_send.at[slot - 1], r_recv.at[slot - 1], to)

    def chip_copy(k, to):
        return send(cpack, cbuf.at[2 * k], c_send.at[k], c_recv.at[k], to)

    def forward(k):
        return send(cbuf.at[2 * k], cbuf.at[2 * k + 1], f_send.at[k], f_recv.at[k], mate)

    def relay(k):
        chip_copy(k, mate).wait_recv()
        forward(k).start()

    own_copies = [send(cpack, cbuf.at[1], c_send.at[0], c_recv.at[0], mate)]
    own_copies += [chip_copy(k, chip_to(k)) for k in range(1, CHIPS)]
    row_copies = [row_copy(slot, row_to(slot)) for slot in range(1, ROWS)]
    for copy in row_copies[:1] + own_copies[:1] + row_copies[1:] + own_copies[1:]:
        copy.start()

    eye = jnp.where(
        lax.broadcasted_iota(jnp.int32, (128, 128), 0) == lax.broadcasted_iota(jnp.int32, (128, 128), 1), 1.0, 0.0
    ).astype(BF16)
    accb[...] = jnp.zeros(accb.shape, F32)
    accx[...] = jnp.zeros(accx.shape, F32)

    def column(block, slot):
        prep_column(block, slot * B, eye, fct, wct, dmat, xmat)

    def row_in(slot):
        row_copy(slot, mate).wait_recv()
        prep_row(rbuf.at[slot - 1], slot * B, frm, wrm)

    def chip_in(k):
        column(cbuf.at[2 * k], 2 * k)
        forward(k).wait_recv()
        column(cbuf.at[2 * k + 1], 2 * k + 1)

    TR = UNIT_R * B

    def tile(u, first, width):
        rs = pl.ds(pl.multiple_of(u * TR, TR), TR)
        cs = pl.ds(pl.multiple_of(first, 2 * B), width)
        value = jnp.exp2(dot(fct[cs, :], frm[:, rs]))
        h, l = split(value)
        accb[:, rs] += dot(dmat[:, cs], h)
        accb[0:32, rs] += dot(dmat[0:32, cs], l)
        h, l = split(value * dot(wct[cs, :], wrm[:, rs]))
        accx[:, rs] += dot(xmat[:, cs], h)
        accx[0:MXL, rs] += dot(xmat[0:MXL, cs], l)

    column(cpack, 0)
    prep_row(rpack, 0, frm, wrm)
    own_copies[0].wait_recv()
    column(cbuf.at[1], 1)
    row_in(1)
    UNITS = ROWS // UNIT_R

    def pass_own(u, carry):
        tile(u, 0, 2 * B)

        @pl.when(u < UNITS - 1)
        def _():
            row_in(2 * u + 2)
            row_in(2 * u + 3)

        @pl.when(u == 2)
        def _():
            relay(1)

        return carry

    lax.fori_loop(0, UNITS, pass_own, 0)
    chip_in(1)

    def pass_one(u, carry):
        @pl.when(u == 0)
        def _():
            relay(2)

        @pl.when(u == 2)
        def _():
            relay(3)

        tile(u, 2 * B, 2 * B)
        return carry

    lax.fori_loop(0, UNITS, pass_one, 0)
    chip_in(2)
    chip_in(3)

    def pass_two(u, carry):
        relay(4 + u)
        tile(u, 4 * B, 4 * B)
        return carry

    lax.fori_loop(0, UNITS, pass_two, 0)
    for k in range(4, CHIPS):
        chip_in(k)

    def ship(slot):
        return send(part.at[slot], red.at[slot - 1], p_send.at[slot - 1], p_recv.at[slot - 1], row_from(slot))

    def pass_last(step, carry):
        u = UNITS - 1 - step

        def half(v, inner):
            tile(u, 8 * B + v * (4 * B), 4 * B)
            return inner

        lax.fori_loop(0, 2, half, 0)
        for j in reversed(range(UNIT_R)):
            slot = u * UNIT_R + j
            cols = pl.ds(pl.multiple_of(slot * B, 128), B)
            y = frm[0:32, cols].astype(F32) + frm[64:96, cols].astype(F32)
            part[slot, 0:DR, :] = accb[0:DR, cols] + accb[DR : 2 * DR, cols]
            weight = accx[0:1, cols]
            first = accx[16:48, cols] + accx[48:80, cols]
            second = accx[80:112, cols] + accx[112:144, cols] + accx[144:176, cols]
            part[slot, DR:PART, :] = y * y * weight - 2.0 * y * first + second
            if j:
                ship(slot).start()
            else:

                @pl.when(u > 0)
                def _():
                    ship(slot).start()

        return carry

    lax.fori_loop(0, UNITS, pass_last, 0)

    d = cpack[48:72, :]
    r = jnp.concatenate([jnp.zeros((1, B), F32), residual[...], jnp.zeros((DR - 18, B), F32)], axis=0)
    product = part[0, 0:DR, :]
    grad = part[0, DR:PART, :]
    for slot in reversed(range(1, ROWS)):
        ship(slot).wait_recv()
        product = product + red[slot - 1, 0:DR, :]
        grad = grad + red[slot - 1, DR:PART, :]
    image = amp[0] * product + noise[0] * d
    ki_out[...] = image
    grad_out[...] = grad

    place = lax.broadcasted_iota(jnp.int32, (DR, 128), 1)
    stats = jnp.zeros((DR, 128), F32)
    for at, value in enumerate((r * r, d * image, r * image, image * image)):
        stats = jnp.where(place == at, jnp.sum(value, axis=1, keepdims=True), stats)
    tot[0] = stats

    def tell_row(slot):
        return send(tot.at[0], statr.at[slot - 1], s_send.at[slot - 1], s_recv.at[slot - 1], row_to(slot))

    def tell_col(o):
        return send(tot.at[1], statc.at[o - 1], t_send.at[o - 1], t_recv.at[o - 1], (row, (col + o) % 16))

    for slot in reversed(range(1, ROWS)):
        tell_row(slot).start()
    for slot in range(1, ROWS):
        tell_row(slot).wait_recv()
        stats = stats + statr[slot - 1]
    tot[1] = stats
    for o in range(1, 2 * CHIPS):
        tell_col(o).start()
    for o in range(1, 2 * CHIPS):
        tell_col(o).wait_recv()
        stats = stats + statc[o - 1]
    stat_out[...] = stats

    for copy in own_copies + row_copies:
        copy.wait_send()
    for k in range(1, CHIPS):
        forward(k).wait_send()
    for slot in range(1, ROWS):
        ship(slot).wait_send()
        tell_row(slot).wait_send()
    for o in range(1, 2 * CHIPS):
        tell_col(o).wait_send()


def on_device(points, lengthscale, outputscale, noise, rhs, iterate, residual, direction):
    systems = rhs.shape[0]
    vmem = pl.BlockSpec(memory_space=pltpu.VMEM)
    smem = pl.BlockSpec(memory_space=pltpu.SMEM)
    points_c = 2 * CHIPS * B
    points_r = ROWS * B
    dma = pltpu.SemaphoreType.DMA
    image, grad, stats = pl.pallas_call(
        kernel,
        out_shape=[
            jax.ShapeDtypeStruct((DR, B), F32),
            jax.ShapeDtypeStruct((32, B), F32),
            jax.ShapeDtypeStruct((DR, 128), F32),
        ],
        in_specs=[vmem, vmem, smem, smem, vmem, vmem, vmem, vmem],
        out_specs=[vmem, vmem, vmem],
        scratch_shapes=[
            pltpu.VMEM((CP, B), F32),
            pltpu.VMEM((RP, B), F32),
            pltpu.VMEM((2 * CHIPS, CP, B), F32),
            pltpu.VMEM((ROWS - 1, RP, B), F32),
            pltpu.VMEM((points_c, 128), BF16),
            pltpu.VMEM((points_c, 128), BF16),
            pltpu.VMEM((MB, points_c), BF16),
            pltpu.VMEM((MX, points_c), BF16),
            pltpu.VMEM((128, points_r), BF16),
            pltpu.VMEM((128, points_r), BF16),
            pltpu.VMEM((MB, points_r), F32),
            pltpu.VMEM((MX, points_r), F32),
            pltpu.VMEM((ROWS, PART, B), F32),
            pltpu.VMEM((ROWS - 1, PART, B), F32),
            pltpu.VMEM((ROWS - 1, DR, 128), F32),
            pltpu.VMEM((2 * CHIPS - 1, DR, 128), F32),
            pltpu.VMEM((2, DR, 128), F32),
            dma((CHIPS,)),
            dma((CHIPS,)),
            dma((CHIPS,)),
            dma((CHIPS,)),
            dma((ROWS - 1,)),
            dma((ROWS - 1,)),
            dma((ROWS - 1,)),
            dma((ROWS - 1,)),
            dma((ROWS - 1,)),
            dma((ROWS - 1,)),
            dma((2 * CHIPS - 1,)),
            dma((2 * CHIPS - 1,)),
        ],
        compiler_params=pltpu.CompilerParams(
            collective_id=0, has_side_effects=True, vmem_limit_bytes=56 << 20
        ),
        name="cg_step",
    )(points, lengthscale[None, :], outputscale, noise, rhs, iterate, residual, direction)

    live = slice(1, 1 + systems)
    image = image[live]
    norm_now, curvature, cross, square = (stats[live, j : j + 1] for j in range(4))
    step = norm_now / curvature
    norm_next = jnp.maximum(norm_now - 2.0 * step * cross + step * step * square, 0.0)
    residual_next = residual - step * image
    iterate_next = iterate + step * direction
    direction_next = residual_next + (norm_next / (norm_now + 1e-06)) * direction
    length_terms = ((0.5 / LOG2E) * outputscale[0] / lengthscale)[:, None] * grad
    return (iterate_next, residual_next, direction_next, length_terms)


def solution(mesh):
    spread = P(None, ("row", "col"))
    return jax.shard_map(
        on_device,
        mesh=mesh,
        in_specs=(spread, P(), P(), P(), spread, spread, spread, spread),
        out_specs=(spread, spread, spread, spread),
        check_vma=False,
    )
```

```python
import functools
import math

import jax
import jax.numpy as jnp
from jax import lax
from jax.experimental import pallas as pl
from jax.experimental.pallas import tpu as pltpu
from jax.sharding import PartitionSpec as P

F32 = jnp.float32
BF16 = jnp.bfloat16
MESH = pl.DeviceIdType.MESH
LOG2E = math.log2(math.e)

ROWS = 8
CHIPS = 8
B = 384
UNIT_R = 2
CP = 72
RP = 56
DR = 24
MB = 48
MX = 176
MXL = 144
PART = 56


def dot(a, b):
    return lax.dot_general(a, b, (((1,), (0,)), ((), ())), preferred_element_type=F32)


def high(v):
    return v.astype(BF16).astype(F32)


def split(v):
    h = v.astype(BF16)
    return h, (v - h.astype(F32)).astype(BF16)


def norm_rows(first, second):
    lane = lax.broadcasted_iota(jnp.int32, (8, B), 0)
    s = -0.5 * jnp.sum(first * first + 2.0 * first * second, axis=0, keepdims=True)
    s0 = high(s)
    s1 = high(s - s0)
    s2 = s - s0 - s1
    parts = jnp.where(lane % 3 == 0, s0, jnp.where(lane % 3 == 1, s1, s2))
    return lane, parts


def prep_column(block, at, eye, fct, wct, dmat, xmat):
    y = block[0:32, :]
    yh = high(y)
    yl = high(y - yh)
    lane, parts = norm_rows(yh, yl)
    tail = jnp.where(lane < 3, parts, jnp.where(lane < 6, 1.0, 0.0))
    zeros = jnp.zeros((24, B), F32)
    c = block[32:56, :]
    ch = high(c)
    cl = c - ch
    feats = jnp.concatenate([yh, yl, yh, tail, zeros], axis=0).astype(BF16)
    wfeat = jnp.concatenate([ch, cl, ch, jnp.zeros((56, B), F32)], axis=0).astype(BF16)
    both = jnp.concatenate([feats, wfeat], axis=0)
    for j in range(B // 128):
        turned = lax.dot_general(
            eye, both[:, j * 128 : (j + 1) * 128], (((1,), (1,)), ((), ())), preferred_element_type=F32
        ).astype(BF16)
        rows = pl.ds(pl.multiple_of(at + j * 128, 128), 128)
        fct[rows, :] = turned[:, :128]
        wct[rows, :] = turned[:, 128:]
    cols = pl.ds(pl.multiple_of(at, 128), B)
    d = block[48:72, :]
    dh = high(d)
    dmat[:, cols] = jnp.concatenate([dh, d - dh], axis=0).astype(BF16)
    exact = yh + yl
    q = exact * exact
    q0 = high(q)
    q1 = high(q - q0)
    q2 = q - q0 - q1
    one = jnp.where(lax.broadcasted_iota(jnp.int32, (16, B), 0) == 0, 1.0, 0.0)
    xmat[:, cols] = jnp.concatenate([one, yh, yl, q0, q1, q2], axis=0).astype(BF16)


def prep_row(block, at, frm, wrm):
    y = block[0:32, :]
    yh = high(y)
    yl = high(y - yh)
    lane, parts = norm_rows(yh, yl)
    tail = jnp.where(lane < 3, 1.0, jnp.where(lane < 6, parts, 0.0))
    cols = pl.ds(pl.multiple_of(at, 128), B)
    frm[:, cols] = jnp.concatenate([yh, yh, yl, tail, jnp.zeros((24, B), F32)], axis=0).astype(BF16)
    c = block[32:56, :]
    ch = high(c)
    wrm[:, cols] = jnp.concatenate([ch, ch, c - ch, jnp.zeros((56, B), F32)], axis=0).astype(BF16)


ROW_STEPS = ((0, 0), (1, 0), (3, 0), (2, 0), (0, 1), (1, 1), (3, 1), (2, 1))
CHIP_STEPS = ((0, 0), (1, 0), (3, 0), (0, 1), (2, 0), (1, 1), (3, 1), (2, 1))


def kernel(
    points, lengths, amp, noise, rhs, iterate, residual, direction, iterate_out, residual_out, direction_out, terms_out,
    cpack, rpack, cbuf, rbuf, fct, wct, dmat, xmat, frm, wrm, accb, accx, part, red, statr, statc, tot,
    c_send, c_recv, f_send, f_recv, r_send, r_recv, p_send, p_recv, s_send, s_recv, t_send, t_recv,
):
    row = lax.axis_index("row")
    col = lax.axis_index("col")
    core = col % 2
    x = (col // 2) % 4
    z = col // 8
    mate = (row, z * 8 + x * 2 + (1 - core))

    def chip_to(k):
        dx, dz = CHIP_STEPS[k]
        return (row, ((z + dz) % 2) * 8 + ((x + dx) % 4) * 2 + core)

    def row_to(slot):
        dy, dz = ROW_STEPS[slot]
        return (((row // 2 + dy) % 4) * 2 + (row + dz) % 2, col)

    def row_from(slot):
        turn = slot % 4
        dy = turn + (turn // 2) * (1 - 2 * (turn % 2))
        return (((row // 2 + 4 - dy) % 4) * 2 + (row + slot // 4) % 2, col)

    barrier = pltpu.get_barrier_semaphore()
    for slot in range(1, ROWS):
        pl.semaphore_signal(barrier, inc=1, device_id=row_to(slot), device_id_type=MESH)
    for o in range(1, 2 * CHIPS):
        pl.semaphore_signal(barrier, inc=1, device_id=(row, (col + o) % 16), device_id_type=MESH)

    wide = jnp.broadcast_to(lengths[...], (32, 32))
    diagonal = lax.broadcasted_iota(jnp.int32, (32, 32), 0) == lax.broadcasted_iota(jnp.int32, (32, 32), 1)
    length = jnp.sum(jnp.where(diagonal, wide, 0.0), axis=1, keepdims=True)
    y = points[...] * (math.sqrt(LOG2E) / length)
    rpack[0:32, :] = y
    rpack[32:48, :] = iterate[1:17, :]
    rpack[48:49, :] = iterate[0:1, :]
    rpack[49:RP, :] = jnp.zeros((RP - 49, B), F32)
    cpack[0:32, :] = y
    cpack[32:48, :] = rhs[1:17, :] * (-1.0 / 16.0)
    cpack[48:49, :] = iterate[0:1, :]
    cpack[49:66, :] = direction[...]
    cpack[66:CP, :] = jnp.zeros((CP - 66, B), F32)
    pl.semaphore_wait(barrier, ROWS - 1 + 2 * CHIPS - 1)

    def send(src, dst, ssem, rsem, to):
        return pltpu.make_async_remote_copy(
            src_ref=src, dst_ref=dst, send_sem=ssem, recv_sem=rsem, device_id=to, device_id_type=MESH
        )

    def row_copy(slot, to):
        return send(rpack, rbuf.at[slot - 1], r_send.at[slot - 1], r_recv.at[slot - 1], to)

    def chip_copy(k, to):
        return send(cpack, cbuf.at[2 * k], c_send.at[k], c_recv.at[k], to)

    def forward(k):
        return send(cbuf.at[2 * k], cbuf.at[2 * k + 1], f_send.at[k], f_recv.at[k], mate)

    def relay(k):
        chip_copy(k, mate).wait_recv()
        forward(k).start()

    own_copies = [send(cpack, cbuf.at[1], c_send.at[0], c_recv.at[0], mate)]
    own_copies += [chip_copy(k, chip_to(k)) for k in range(1, CHIPS)]
    row_copies = [row_copy(slot, row_to(slot)) for slot in range(1, ROWS)]
    for copy in row_copies[:1] + own_copies[:1] + row_copies[1:] + own_copies[1:]:
        copy.start()

    eye = jnp.where(
        lax.broadcasted_iota(jnp.int32, (128, 128), 0) == lax.broadcasted_iota(jnp.int32, (128, 128), 1), 1.0, 0.0
    ).astype(BF16)
    accb[...] = jnp.zeros(accb.shape, F32)
    accx[...] = jnp.zeros(accx.shape, F32)

    def column(block, slot):
        prep_column(block, slot * B, eye, fct, wct, dmat, xmat)

    def row_in(slot):
        row_copy(slot, mate).wait_recv()
        prep_row(rbuf.at[slot - 1], slot * B, frm, wrm)

    def chip_in(k):
        column(cbuf.at[2 * k], 2 * k)
        forward(k).wait_recv()
        column(cbuf.at[2 * k + 1], 2 * k + 1)

    TR = UNIT_R * B

    def tile(u, first, width):
        rs = pl.ds(pl.multiple_of(u * TR, TR), TR)
        cs = pl.ds(pl.multiple_of(first, 2 * B), width)
        value = jnp.exp2(dot(fct[cs, :], frm[:, rs]))
        h, l = split(value)
        accb[:, rs] += dot(dmat[:, cs], h)
        accb[0:32, rs] += dot(dmat[0:32, cs], l)
        h, l = split(value * dot(wct[cs, :], wrm[:, rs]))
        accx[:, rs] += dot(xmat[:, cs], h)
        accx[0:MXL, rs] += dot(xmat[0:MXL, cs], l)

    column(cpack, 0)
    prep_row(rpack, 0, frm, wrm)
    own_copies[0].wait_recv()
    column(cbuf.at[1], 1)
    row_in(1)
    UNITS = ROWS // UNIT_R

    def pass_own(u, carry):
        tile(u, 0, 2 * B)

        @pl.when(u < UNITS - 1)
        def _():
            row_in(2 * u + 2)
            row_in(2 * u + 3)

        @pl.when(u == 2)
        def _():
            relay(1)

        return carry

    lax.fori_loop(0, UNITS, pass_own, 0)
    chip_in(1)

    def pass_one(u, carry):
        @pl.when(u == 0)
        def _():
            relay(2)

        @pl.when(u == 2)
        def _():
            relay(3)

        tile(u, 2 * B, 2 * B)
        return carry

    lax.fori_loop(0, UNITS, pass_one, 0)
    chip_in(2)
    chip_in(3)

    def pass_two(u, carry):
        relay(4 + u)
        tile(u, 4 * B, 4 * B)
        return carry

    lax.fori_loop(0, UNITS, pass_two, 0)
    for k in range(4, CHIPS):
        chip_in(k)

    def ship(slot):
        return send(part.at[slot], red.at[slot - 1], p_send.at[slot - 1], p_recv.at[slot - 1], row_from(slot))

    def pass_last(step, carry):
        u = UNITS - 1 - step

        def half(v, inner):
            tile(u, 8 * B + v * (4 * B), 4 * B)
            return inner

        lax.fori_loop(0, 2, half, 0)
        for j in reversed(range(UNIT_R)):
            slot = u * UNIT_R + j
            cols = pl.ds(pl.multiple_of(slot * B, 128), B)
            y = frm[0:32, cols].astype(F32) + frm[64:96, cols].astype(F32)
            part[slot, 0:DR, :] = accb[0:DR, cols] + accb[DR : 2 * DR, cols]
            weight = accx[0:1, cols]
            first = accx[16:48, cols] + accx[48:80, cols]
            second = accx[80:112, cols] + accx[112:144, cols] + accx[144:176, cols]
            part[slot, DR:PART, :] = y * y * weight - 2.0 * y * first + second
            if j:
                ship(slot).start()
            else:

                @pl.when(u > 0)
                def _():
                    ship(slot).start()

        return carry

    lax.fori_loop(0, UNITS, pass_last, 0)

    d = cpack[48:72, :]
    r = jnp.concatenate([jnp.zeros((1, B), F32), residual[...], jnp.zeros((DR - 18, B), F32)], axis=0)
    product = part[0, 0:DR, :]
    grad = part[0, DR:PART, :]
    for slot in reversed(range(1, ROWS)):
        ship(slot).wait_recv()
        product = product + red[slot - 1, 0:DR, :]
        grad = grad + red[slot - 1, DR:PART, :]
    image = amp[0] * product + noise[0] * d
    terms_out[...] = ((0.5 / LOG2E) * amp[0] / length) * grad

    place = lax.broadcasted_iota(jnp.int32, (8, 128), 0)
    corner = lax.broadcasted_iota(jnp.int32, (DR, 128), 0) == lax.broadcasted_iota(jnp.int32, (DR, 128), 1)
    stats = jnp.zeros((8, 128), F32)
    for at, value in enumerate((r * r, d * image, r * image, image * image)):
        total = jnp.where(corner, jnp.sum(value, axis=1, keepdims=True), 0.0)
        stats = jnp.where(place == at, jnp.sum(total, axis=0, keepdims=True), stats)
    tot[0] = stats

    def tell_row(slot):
        return send(tot.at[0], statr.at[slot - 1], s_send.at[slot - 1], s_recv.at[slot - 1], row_to(slot))

    def tell_col(o):
        return send(tot.at[1], statc.at[o - 1], t_send.at[o - 1], t_recv.at[o - 1], (row, (col + o) % 16))

    for slot in reversed(range(1, ROWS)):
        tell_row(slot).start()
    for slot in range(1, ROWS):
        tell_row(slot).wait_recv()
        stats = stats + statr[slot - 1]
    tot[1] = stats
    for o in range(1, 2 * CHIPS):
        tell_col(o).start()
    for o in range(1, 2 * CHIPS):
        tell_col(o).wait_recv()
        stats = stats + statc[o - 1]

    norm_now, curvature, cross, square = (stats[j : j + 1, :] for j in range(4))
    step = norm_now / curvature
    norm_next = jnp.maximum(norm_now - 2.0 * step * cross + step * step * square, 0.0)
    ratio = norm_next / (norm_now + 1e-06)

    def upright(line):
        return jnp.sum(jnp.where(corner, line, 0.0), axis=1, keepdims=True)[1:18, :]

    step = upright(step)
    residual_next = residual[...] - step * image[1:18, :]
    iterate_out[...] = iterate[...] + step * direction[...]
    residual_out[...] = residual_next
    direction_out[...] = residual_next + upright(ratio) * direction[...]

    for copy in own_copies + row_copies:
        copy.wait_send()
    for k in range(1, CHIPS):
        forward(k).wait_send()
    for slot in range(1, ROWS):
        ship(slot).wait_send()
        tell_row(slot).wait_send()
    for o in range(1, 2 * CHIPS):
        tell_col(o).wait_send()


def on_device(points, lengthscale, outputscale, noise, rhs, iterate, residual, direction):
    vmem = pl.BlockSpec(memory_space=pltpu.VMEM)
    smem = pl.BlockSpec(memory_space=pltpu.SMEM)
    points_c = 2 * CHIPS * B
    points_r = ROWS * B
    dma = pltpu.SemaphoreType.DMA
    return tuple(pl.pallas_call(
        kernel,
        out_shape=[
            jax.ShapeDtypeStruct((17, B), F32),
            jax.ShapeDtypeStruct((17, B), F32),
            jax.ShapeDtypeStruct((17, B), F32),
            jax.ShapeDtypeStruct((32, B), F32),
        ],
        in_specs=[vmem, vmem, smem, smem, vmem, vmem, vmem, vmem],
        out_specs=[vmem, vmem, vmem, vmem],
        scratch_shapes=[
            pltpu.VMEM((CP, B), F32),
            pltpu.VMEM((RP, B), F32),
            pltpu.VMEM((2 * CHIPS, CP, B), F32),
            pltpu.VMEM((ROWS - 1, RP, B), F32),
            pltpu.VMEM((points_c, 128), BF16),
            pltpu.VMEM((points_c, 128), BF16),
            pltpu.VMEM((MB, points_c), BF16),
            pltpu.VMEM((MX, points_c), BF16),
            pltpu.VMEM((128, points_r), BF16),
            pltpu.VMEM((128, points_r), BF16),
            pltpu.VMEM((MB, points_r), F32),
            pltpu.VMEM((MX, points_r), F32),
            pltpu.VMEM((ROWS, PART, B), F32),
            pltpu.VMEM((ROWS - 1, PART, B), F32),
            pltpu.VMEM((ROWS - 1, 8, 128), F32),
            pltpu.VMEM((2 * CHIPS - 1, 8, 128), F32),
            pltpu.VMEM((2, 8, 128), F32),
            dma((CHIPS,)),
            dma((CHIPS,)),
            dma((CHIPS,)),
            dma((CHIPS,)),
            dma((ROWS - 1,)),
            dma((ROWS - 1,)),
            dma((ROWS - 1,)),
            dma((ROWS - 1,)),
            dma((ROWS - 1,)),
            dma((ROWS - 1,)),
            dma((2 * CHIPS - 1,)),
            dma((2 * CHIPS - 1,)),
        ],
        compiler_params=pltpu.CompilerParams(
            collective_id=0, has_side_effects=True, vmem_limit_bytes=56 << 20
        ),
        name="cg_step",
    )(points, lengthscale[None, :], outputscale, noise, rhs, iterate, residual, direction))


def solution(mesh):
    spread = P(None, ("row", "col"))
    return jax.shard_map(
        on_device,
        mesh=mesh,
        in_specs=(spread, P(), P(), P(), spread, spread, spread, spread),
        out_specs=(spread, spread, spread, spread),
        check_vma=False,
    )
```

```python
import functools
import math

import jax
import jax.numpy as jnp
from jax import lax
from jax.experimental import pallas as pl
from jax.experimental.pallas import tpu as pltpu
from jax.sharding import PartitionSpec as P

F32 = jnp.float32
BF16 = jnp.bfloat16
MESH = pl.DeviceIdType.MESH
LOG2E = math.log2(math.e)

ROWS = 8
CHIPS = 8
B = 384
UNIT_R = 2
CP = 72
RP = 56
DR = 24
MB = 48
MX = 176
MXL = 144
LATE = 2


def dot(a, b):
    return lax.dot_general(a, b, (((1,), (0,)), ((), ())), preferred_element_type=F32)


def high(v):
    return v.astype(BF16).astype(F32)


def split(v):
    h = v.astype(BF16)
    return h, (v - h.astype(F32)).astype(BF16)


def norm_rows(first, second):
    lane = lax.broadcasted_iota(jnp.int32, (8, B), 0)
    s = -0.5 * jnp.sum(first * first + 2.0 * first * second, axis=0, keepdims=True)
    s0 = high(s)
    s1 = high(s - s0)
    s2 = s - s0 - s1
    parts = jnp.where(lane % 3 == 0, s0, jnp.where(lane % 3 == 1, s1, s2))
    return lane, parts


def prep_column(block, at, eye, fct, wct, dmat, xmat):
    y = block[0:32, :]
    yh = high(y)
    yl = high(y - yh)
    lane, parts = norm_rows(yh, yl)
    tail = jnp.where(lane < 3, parts, jnp.where(lane < 6, 1.0, 0.0))
    zeros = jnp.zeros((24, B), F32)
    c = block[32:56, :]
    ch = high(c)
    cl = c - ch
    feats = jnp.concatenate([yh, yl, yh, tail, zeros], axis=0).astype(BF16)
    wfeat = jnp.concatenate([ch, cl, ch, jnp.zeros((56, B), F32)], axis=0).astype(BF16)
    both = jnp.concatenate([feats, wfeat], axis=0)
    for j in range(B // 128):
        turned = lax.dot_general(
            eye, both[:, j * 128 : (j + 1) * 128], (((1,), (1,)), ((), ())), preferred_element_type=F32
        ).astype(BF16)
        rows = pl.ds(pl.multiple_of(at + j * 128, 128), 128)
        fct[rows, :] = turned[:, :128]
        wct[rows, :] = turned[:, 128:]
    cols = pl.ds(pl.multiple_of(at, 128), B)
    d = block[48:72, :]
    dh = high(d)
    dmat[:, cols] = jnp.concatenate([dh, d - dh], axis=0).astype(BF16)
    exact = yh + yl
    q = exact * exact
    q0 = high(q)
    q1 = high(q - q0)
    q2 = q - q0 - q1
    one = jnp.where(lax.broadcasted_iota(jnp.int32, (16, B), 0) == 0, 1.0, 0.0)
    xmat[:, cols] = jnp.concatenate([one, yh, yl, q0, q1, q2], axis=0).astype(BF16)


def prep_row(block, at, frm, wrm):
    y = block[0:32, :]
    yh = high(y)
    yl = high(y - yh)
    lane, parts = norm_rows(yh, yl)
    tail = jnp.where(lane < 3, 1.0, jnp.where(lane < 6, parts, 0.0))
    cols = pl.ds(pl.multiple_of(at, 128), B)
    frm[:, cols] = jnp.concatenate([yh, yh, yl, tail, jnp.zeros((24, B), F32)], axis=0).astype(BF16)
    c = block[32:56, :]
    ch = high(c)
    wrm[:, cols] = jnp.concatenate([ch, ch, c - ch, jnp.zeros((56, B), F32)], axis=0).astype(BF16)


ROW_STEPS = ((0, 0), (1, 0), (3, 0), (2, 0), (0, 1), (1, 1), (3, 1), (2, 1))
CHIP_STEPS = ((0, 0), (1, 0), (3, 0), (0, 1), (2, 0), (1, 1), (3, 1), (2, 1))


def kernel(
    points, lengths, amp, noise, rhs, iterate, residual, direction, iterate_out, residual_out, direction_out, terms_out,
    cpack, rpack, cbuf, rbuf, fct, wct, dmat, xmat, frm, wrm, accb, accx, keep, partp, partg, redp, redg, statr, statc, tot, image_ref,
    c_send, c_recv, f_send, f_recv, r_send, r_recv, p_send, p_recv, g_send, g_recv, s_send, s_recv, t_send, t_recv,
):
    row = lax.axis_index("row")
    col = lax.axis_index("col")
    core = col % 2
    x = (col // 2) % 4
    z = col // 8
    mate = (row, z * 8 + x * 2 + (1 - core))

    def chip_to(k):
        dx, dz = CHIP_STEPS[k]
        return (row, ((z + dz) % 2) * 8 + ((x + dx) % 4) * 2 + core)

    def row_to(slot):
        dy, dz = ROW_STEPS[slot]
        return (((row // 2 + dy) % 4) * 2 + (row + dz) % 2, col)

    def row_from(slot):
        turn = slot % 4
        dy = turn + (turn // 2) * (1 - 2 * (turn % 2))
        return (((row // 2 + 4 - dy) % 4) * 2 + (row + slot // 4) % 2, col)

    barrier = pltpu.get_barrier_semaphore()
    for slot in range(1, ROWS):
        pl.semaphore_signal(barrier, inc=1, device_id=row_to(slot), device_id_type=MESH)
    for o in range(1, 2 * CHIPS):
        pl.semaphore_signal(barrier, inc=1, device_id=(row, (col + o) % 16), device_id_type=MESH)

    wide = jnp.broadcast_to(lengths[...], (32, 32))
    diagonal = lax.broadcasted_iota(jnp.int32, (32, 32), 0) == lax.broadcasted_iota(jnp.int32, (32, 32), 1)
    length = jnp.sum(jnp.where(diagonal, wide, 0.0), axis=1, keepdims=True)
    y = points[...] * (math.sqrt(LOG2E) / length)
    rpack[0:32, :] = y
    rpack[32:48, :] = iterate[1:17, :]
    rpack[48:49, :] = iterate[0:1, :]
    rpack[49:RP, :] = jnp.zeros((RP - 49, B), F32)
    cpack[0:32, :] = y
    cpack[32:48, :] = rhs[1:17, :] * (-1.0 / 16.0)
    cpack[48:49, :] = iterate[0:1, :]
    cpack[49:66, :] = direction[...]
    cpack[66:CP, :] = jnp.zeros((CP - 66, B), F32)
    pl.semaphore_wait(barrier, ROWS - 1 + 2 * CHIPS - 1)

    def send(src, dst, ssem, rsem, to):
        return pltpu.make_async_remote_copy(
            src_ref=src, dst_ref=dst, send_sem=ssem, recv_sem=rsem, device_id=to, device_id_type=MESH
        )

    def row_copy(slot, to):
        return send(rpack, rbuf.at[slot - 1], r_send.at[slot - 1], r_recv.at[slot - 1], to)

    def chip_copy(k, to):
        return send(cpack, cbuf.at[2 * k], c_send.at[k], c_recv.at[k], to)

    def forward(k):
        return send(cbuf.at[2 * k], cbuf.at[2 * k + 1], f_send.at[k], f_recv.at[k], mate)

    def relay(k):
        chip_copy(k, mate).wait_recv()
        forward(k).start()

    own_copies = [send(cpack, cbuf.at[1], c_send.at[0], c_recv.at[0], mate)]
    own_copies += [chip_copy(k, chip_to(k)) for k in range(1, CHIPS)]
    row_copies = [row_copy(slot, row_to(slot)) for slot in range(1, ROWS)]
    for copy in row_copies[:1] + own_copies[:1] + row_copies[1:] + own_copies[1:]:
        copy.start()

    eye = jnp.where(
        lax.broadcasted_iota(jnp.int32, (128, 128), 0) == lax.broadcasted_iota(jnp.int32, (128, 128), 1), 1.0, 0.0
    ).astype(BF16)
    accb[...] = jnp.zeros(accb.shape, F32)
    accx[...] = jnp.zeros(accx.shape, F32)

    def column(block, slot):
        prep_column(block, slot * B, eye, fct, wct, dmat, xmat)

    def row_in(slot):
        row_copy(slot, mate).wait_recv()
        prep_row(rbuf.at[slot - 1], slot * B, frm, wrm)

    def chip_in(k):
        column(cbuf.at[2 * k], 2 * k)
        forward(k).wait_recv()
        column(cbuf.at[2 * k + 1], 2 * k + 1)

    TR = UNIT_R * B

    def tile(u, first, width):
        rs = pl.ds(pl.multiple_of(u * TR, TR), TR)
        cs = pl.ds(pl.multiple_of(first, 2 * B), width)
        value = jnp.exp2(dot(fct[cs, :], frm[:, rs]))
        h, l = split(value)
        accb[:, rs] += dot(dmat[:, cs], h)
        accb[0:32, rs] += dot(dmat[0:32, cs], l)
        h, l = split(value * dot(wct[cs, :], wrm[:, rs]))
        accx[:, rs] += dot(xmat[:, cs], h)
        accx[0:MXL, rs] += dot(xmat[0:MXL, cs], l)

    column(cpack, 0)
    prep_row(rpack, 0, frm, wrm)
    own_copies[0].wait_recv()
    column(cbuf.at[1], 1)
    row_in(1)
    UNITS = ROWS // UNIT_R

    def pass_own(u, carry):
        tile(u, 0, 2 * B)

        @pl.when(u < UNITS - 1)
        def _():
            row_in(2 * u + 2)
            row_in(2 * u + 3)

        @pl.when(u == 2)
        def _():
            relay(1)

        return carry

    lax.fori_loop(0, UNITS, pass_own, 0)
    chip_in(1)

    def pass_one(u, carry):
        @pl.when(u == 0)
        def _():
            relay(2)

        @pl.when(u == 2)
        def _():
            relay(3)

        tile(u, 2 * B, 2 * B)
        return carry

    lax.fori_loop(0, UNITS, pass_one, 0)
    chip_in(2)
    chip_in(3)

    def pass_two(u, carry):
        relay(4 + u)
        tile(u, 4 * B, 4 * B)
        return carry

    lax.fori_loop(0, UNITS, pass_two, 0)
    for k in range(4, CHIPS):
        chip_in(k)

    def tile_product(u, v, rs, cs):
        value = jnp.exp2(dot(fct[cs, :], frm[:, rs]))
        keep[2 * u + v] = value
        h, l = split(value)
        accb[:, rs] += dot(dmat[:, cs], h)
        accb[0:32, rs] += dot(dmat[0:32, cs], l)

    def tile_gradient(u, v, rs, cs):
        h, l = split(keep[2 * u + v] * dot(wct[cs, :], wrm[:, rs]))
        accx[:, rs] += dot(xmat[:, cs], h)
        accx[0:MXL, rs] += dot(xmat[0:MXL, cs], l)

    def halves(u, work):
        def half(v, inner):
            rs = pl.ds(pl.multiple_of(u * TR, TR), TR)
            cs = pl.ds(pl.multiple_of(8 * B + v * (4 * B), 4 * B), 4 * B)
            work(u, v, rs, cs)
            return inner

        lax.fori_loop(0, 2, half, 0)

    def ship_product(slot):
        return send(partp.at[slot], redp.at[slot - 1], p_send.at[slot - 1], p_recv.at[slot - 1], row_from(slot))

    def ship_gradient(slot):
        return send(partg.at[slot], redg.at[slot - 1], g_send.at[slot - 1], g_recv.at[slot - 1], row_from(slot))

    def ship(copy, slot, j, u):
        if j:
            copy(slot).start()
        else:

            @pl.when(u > 0)
            def _():
                copy(slot).start()

    def products_out(u):
        for j in reversed(range(UNIT_R)):
            slot = u * UNIT_R + j
            cols = pl.ds(pl.multiple_of(slot * B, 128), B)
            partp[slot] = accb[0:DR, cols] + accb[DR : 2 * DR, cols]
            ship(ship_product, slot, j, u)

    def gradients_out(u):
        for j in reversed(range(UNIT_R)):
            slot = u * UNIT_R + j
            cols = pl.ds(pl.multiple_of(slot * B, 128), B)
            y = frm[0:32, cols].astype(F32) + frm[64:96, cols].astype(F32)
            weight = accx[0:1, cols]
            first = accx[16:48, cols] + accx[48:80, cols]
            second = accx[80:112, cols] + accx[112:144, cols] + accx[144:176, cols]
            partg[slot] = y * y * weight - 2.0 * y * first + second
            ship(ship_gradient, slot, j, u)

    def pass_last(step, carry):
        u = UNITS - 1 - step
        halves(u, lambda u, v, rs, cs: tile(u, 8 * B + v * (4 * B), 4 * B))
        products_out(u)
        gradients_out(u)
        return carry

    def pass_product(step, carry):
        u = LATE - 1 - step
        halves(u, tile_product)
        products_out(u)
        return carry

    def pass_gradient(step, carry):
        u = LATE - 1 - step
        halves(u, tile_gradient)
        gradients_out(u)
        return carry

    lax.fori_loop(0, UNITS - LATE, pass_last, 0)
    lax.fori_loop(0, LATE, pass_product, 0)
    lax.fori_loop(0, LATE - 1, pass_gradient, 0)

    d = cpack[48:72, :]
    r = jnp.concatenate([jnp.zeros((1, B), F32), residual[...], jnp.zeros((DR - 18, B), F32)], axis=0)
    product = partp[0]
    for slot in reversed(range(1, ROWS)):
        ship_product(slot).wait_recv()
        product = product + redp[slot - 1]
    image = amp[0] * product + noise[0] * d
    image_ref[...] = image

    place = lax.broadcasted_iota(jnp.int32, (8, 128), 0)
    corner = lax.broadcasted_iota(jnp.int32, (DR, 128), 0) == lax.broadcasted_iota(jnp.int32, (DR, 128), 1)
    stats = jnp.zeros((8, 128), F32)
    for at, value in enumerate((r * r, d * image, r * image, image * image)):
        total = jnp.where(corner, jnp.sum(value, axis=1, keepdims=True), 0.0)
        stats = jnp.where(place == at, jnp.sum(total, axis=0, keepdims=True), stats)
    tot[0] = stats

    def tell_row(slot):
        return send(tot.at[0], statr.at[slot - 1], s_send.at[slot - 1], s_recv.at[slot - 1], row_to(slot))

    def tell_col(o):
        return send(tot.at[1], statc.at[o - 1], t_send.at[o - 1], t_recv.at[o - 1], (row, (col + o) % 16))

    for slot in reversed(range(1, ROWS)):
        tell_row(slot).start()
    lax.fori_loop(LATE - 1, LATE, pass_gradient, 0)
    stats = tot[0]
    for slot in range(1, ROWS):
        tell_row(slot).wait_recv()
        stats = stats + statr[slot - 1]
    tot[1] = stats
    for o in range(1, 2 * CHIPS):
        tell_col(o).start()

    grad = partg[0]
    for slot in reversed(range(1, ROWS)):
        ship_gradient(slot).wait_recv()
        grad = grad + redg[slot - 1]
    terms_out[...] = ((0.5 / LOG2E) * amp[0] / length) * grad
    stats = tot[1]
    for o in range(1, 2 * CHIPS):
        tell_col(o).wait_recv()
        stats = stats + statc[o - 1]

    norm_now, curvature, cross, square = (stats[j : j + 1, :] for j in range(4))
    step = norm_now / curvature
    norm_next = jnp.maximum(norm_now - 2.0 * step * cross + step * step * square, 0.0)
    ratio = norm_next / (norm_now + 1e-06)

    def upright(line):
        return jnp.sum(jnp.where(corner, line, 0.0), axis=1, keepdims=True)[1:18, :]

    step = upright(step)
    residual_next = residual[...] - step * image_ref[1:18, :]
    iterate_out[...] = iterate[...] + step * direction[...]
    residual_out[...] = residual_next
    direction_out[...] = residual_next + upright(ratio) * direction[...]

    for copy in own_copies + row_copies:
        copy.wait_send()
    for k in range(1, CHIPS):
        forward(k).wait_send()
    for slot in range(1, ROWS):
        ship_product(slot).wait_send()
        ship_gradient(slot).wait_send()
        tell_row(slot).wait_send()
    for o in range(1, 2 * CHIPS):
        tell_col(o).wait_send()


def on_device(points, lengthscale, outputscale, noise, rhs, iterate, residual, direction):
    vmem = pl.BlockSpec(memory_space=pltpu.VMEM)
    smem = pl.BlockSpec(memory_space=pltpu.SMEM)
    points_c = 2 * CHIPS * B
    points_r = ROWS * B
    dma = pltpu.SemaphoreType.DMA
    return tuple(pl.pallas_call(
        kernel,
        out_shape=[
            jax.ShapeDtypeStruct((17, B), F32),
            jax.ShapeDtypeStruct((17, B), F32),
            jax.ShapeDtypeStruct((17, B), F32),
            jax.ShapeDtypeStruct((32, B), F32),
        ],
        in_specs=[vmem, vmem, smem, smem, vmem, vmem, vmem, vmem],
        out_specs=[vmem, vmem, vmem, vmem],
        scratch_shapes=[
            pltpu.VMEM((CP, B), F32),
            pltpu.VMEM((RP, B), F32),
            pltpu.VMEM((2 * CHIPS, CP, B), F32),
            pltpu.VMEM((ROWS - 1, RP, B), F32),
            pltpu.VMEM((points_c, 128), BF16),
            pltpu.VMEM((points_c, 128), BF16),
            pltpu.VMEM((MB, points_c), BF16),
            pltpu.VMEM((MX, points_c), BF16),
            pltpu.VMEM((128, points_r), BF16),
            pltpu.VMEM((128, points_r), BF16),
            pltpu.VMEM((MB, points_r), F32),
            pltpu.VMEM((MX, points_r), F32),
            pltpu.VMEM((2 * LATE, 4 * B, UNIT_R * B), F32),
            pltpu.VMEM((ROWS, DR, B), F32),
            pltpu.VMEM((ROWS, 32, B), F32),
            pltpu.VMEM((ROWS - 1, DR, B), F32),
            pltpu.VMEM((ROWS - 1, 32, B), F32),
            pltpu.VMEM((ROWS - 1, 8, 128), F32),
            pltpu.VMEM((2 * CHIPS - 1, 8, 128), F32),
            pltpu.VMEM((2, 8, 128), F32),
            pltpu.VMEM((DR, B), F32),
            dma((CHIPS,)),
            dma((CHIPS,)),
            dma((CHIPS,)),
            dma((CHIPS,)),
            dma((ROWS - 1,)),
            dma((ROWS - 1,)),
            dma((ROWS - 1,)),
            dma((ROWS - 1,)),
            dma((ROWS - 1,)),
            dma((ROWS - 1,)),
            dma((ROWS - 1,)),
            dma((ROWS - 1,)),
            dma((2 * CHIPS - 1,)),
            dma((2 * CHIPS - 1,)),
        ],
        compiler_params=pltpu.CompilerParams(
            collective_id=0, has_side_effects=True, vmem_limit_bytes=60 << 20
        ),
        name="cg_step",
    )(points, lengthscale[None, :], outputscale, noise, rhs, iterate, residual, direction))


def solution(mesh):
    spread = P(None, ("row", "col"))
    return jax.shard_map(
        on_device,
        mesh=mesh,
        in_specs=(spread, P(), P(), P(), spread, spread, spread, spread),
        out_specs=(spread, spread, spread, spread),
        check_vma=False,
    )
```
